32 devices in a mesh: stream: 8 (over y, x, core), tp: 4 (over z).
Axes of the slice: x: 2, y: 2, z: 4, core: 2. Of those that a mesh axis runs over, the one named last changes fastest.
Arguments:
- tokens: bfloat16 [12288, 3072], P('stream', 'tp'), may hold values from -6 to 6
- qkv_weight: bfloat16 [3072, 3, 2048], P('stream', None, 'tp'), may hold values from -0.109375 to 0.109375
- gate_weight: bfloat16 [3072, 2048], P('stream', 'tp'), may hold values from -0.109375 to 0.109375
- out_weight: bfloat16 [2048, 3072], P('tp', 'stream'), may hold values from -0.125 to 0.125
- log_decay: float32 [32, 12288], P('tp', 'stream'), may hold values from -1 to 0
- states: float32 [96, 32, 64, 64], P('stream', 'tp'), may hold values from -48 to 48
- dest_slot: int32 [96], P('stream'), may hold values from 0 to 95, as said below
- valid: int32 [96], P('stream'), may hold values from 1 to 128
Outputs:
- mixed: bfloat16 [12288, 3072], P('stream', 'tp')
- new_states: float32 [96, 32, 64, 64], P('stream', 'tp')
The draws below stay inside these ranges and needn't reach their ends.
Inputs may be any that keep to these rules, and one draw needn't show every extreme that they name: dest_slot is a permutation of the streams; of the 12 streams of one device, at most 2 have new positions on any one device, and that many do for some pair of devices.
All inputs are finite; a program needn't handle non-finite values.
Results may differ from the reference program's by a relative error of at most 0.0058.
Values may be sent and summed in bfloat16 or wider, within the bound.
A program may use at most 128 MiB of HBM per device.

```python
import math
import jax
import jax.numpy as jnp
from jax import lax

D = 3072
NUM_ATTENDERS = 32
HD = 64
WINDOW_LENGTH = 128
SD = 12
NUM_SEQUENCES = 96
TOKENS = 12288


def draw_log_decay(key, part):
    lookup_vectors = jax.random.split(key, 5)
    forgetting_speed = jnp.exp(jax.random.uniform(lookup_vectors[0], (NUM_ATTENDERS, 1, 1), jnp.float32, math.log(0.2 / WINDOW_LENGTH), math.log(1.0 / 30.0)))
    multiplier_value = jnp.exp(jax.random.uniform(lookup_vectors[1], (1, NUM_SEQUENCES, 1), jnp.float32, math.log(0.5), math.log(2.0)))
    noise_offset = jax.random.uniform(lookup_vectors[2], (NUM_ATTENDERS, NUM_SEQUENCES, WINDOW_LENGTH), jnp.float32, 0.6, 1.4)
    sequence_bundles = jax.random.bernoulli(lookup_vectors[3], 2.0 / WINDOW_LENGTH, (NUM_ATTENDERS, NUM_SEQUENCES, WINDOW_LENGTH)).astype(jnp.float32)
    network_level = jax.random.uniform(lookup_vectors[4], (NUM_ATTENDERS, NUM_SEQUENCES, WINDOW_LENGTH), jnp.float32, 0.22, 0.69)
    overall_number = forgetting_speed * multiplier_value * noise_offset + sequence_bundles * network_level
    return (-overall_number).reshape(NUM_ATTENDERS, NUM_SEQUENCES * WINDOW_LENGTH).astype(jnp.float32)


def draw_dest_slot(key, part):
    node_count = NUM_SEQUENCES // SD
    lookup_vectors = jax.random.split(key, 3)
    first_perm = jax.random.permutation(lookup_vectors[0], node_count)
    second_perm = jax.random.permutation(lookup_vectors[1], node_count)
    slot_keys = jax.random.split(lookup_vectors[2], node_count)
    slot_perm = jax.vmap(lambda k: jax.random.permutation(k, SD))(slot_keys)
    index = jnp.arange(NUM_SEQUENCES, dtype=jnp.int32)
    device = index // SD
    within = index % SD
    target = second_perm[(first_perm[device] + within) % node_count]
    return (target * SD + slot_perm[target, within]).astype(jnp.int32)


def draw_valid(key, part):
    lookup_vectors = jax.random.split(key, 3)
    counts = jax.random.randint(lookup_vectors[0], (NUM_SEQUENCES,), 1, WINDOW_LENGTH + 1, dtype=jnp.int32)
    first_pos = jax.random.randint(lookup_vectors[1], (), 0, NUM_SEQUENCES, dtype=jnp.int32)
    second_pos = (first_pos + 1 + jax.random.randint(lookup_vectors[2], (), 0, NUM_SEQUENCES - 1, dtype=jnp.int32)) % NUM_SEQUENCES
    return counts.at[first_pos].set(WINDOW_LENGTH).at[second_pos].set(1).astype(jnp.int32)


def steps_of(rng, shape, shards, low, top_value):
    def one(position, parts):
        draws = jax.random.uniform(jax.random.fold_in(jax.random.fold_in(rng, 6), position), (parts,), jnp.float32, low / len(shards), top_value / len(shards))
        return jnp.repeat(jnp.exp(draws), shape[position] // parts).reshape((-1,) + (1,) * (len(shape) - position - 1))

    factor_of = one(*shards[0])
    for cut in shards[1:]:
        factor_of = factor_of * one(*cut)
    return factor_of


def noise(own_key, shape, width, limit, shards=(), kind=jnp.bfloat16):
    values = jax.random.normal(own_key, shape, jnp.float32) * width
    if len(shards) > 0:
        values = steps_of(own_key, shape, shards, -0.22, 0.18) * values
    return jnp.clip(values, min=-limit, max=limit).astype(kind)


def setup_inputs(seed: int = 0) -> dict:
    splits = jax.random.split(jax.random.key(seed), 9)
    tokens = noise(splits[0], (TOKENS, D), 1.0, 6.0, ((0, 8), (1, 4)))
    qkv_weight = noise(splits[1], (D, 3, NUM_ATTENDERS * HD), D ** -0.5, 0.109375, ((0, 8), (2, 4)))
    gate_weight = noise(splits[2], (D, NUM_ATTENDERS * HD), D ** -0.5, 0.109375, ((0, 8), (1, 4)))
    out_weight = noise(splits[3], (NUM_ATTENDERS * HD, D), (NUM_ATTENDERS * HD) ** -0.5, 0.125, ((0, 4), (1, 8)))
    log_decay = draw_log_decay(jax.random.fold_in(splits[8], 71), 0)
    states = noise(splits[5], (NUM_SEQUENCES, NUM_ATTENDERS, HD, HD), 8.0, 48.0, ((0, 8), (1, 4)), jnp.float32)
    dest_slot = draw_dest_slot(jax.random.fold_in(splits[8], 71), 0)
    valid = draw_valid(jax.random.fold_in(splits[8], 71), 0)
    return {"tokens": tokens, "qkv_weight": qkv_weight, "gate_weight": gate_weight, "out_weight": out_weight, "log_decay": log_decay, "states": states, "dest_slot": dest_slot, "valid": valid}


def core(projected, gate_sum, decay_log, old_state, valid_rows):
    streams = old_state.shape[0]
    heads = old_state.shape[1]
    rows = projected.shape[0]
    length = rows // streams
    activated = jax.nn.silu(projected).astype(jnp.bfloat16).reshape(streams, length, 3, heads, HD)
    positions = jnp.arange(length, dtype=jnp.int32)
    live = positions[None, :] < valid_rows[:, None]
    live_half = live.astype(jnp.bfloat16)[:, :, None, None]
    live_full = live.astype(jnp.float32)
    query = activated[:, :, 0]
    lookup_vectors = activated[:, :, 1] * live_half
    values = activated[:, :, 2] * live_half
    decay = decay_log.reshape(heads, streams, length).transpose(1, 0, 2) * live_full[:, None, :]
    cumulative = jnp.cumsum(decay, axis=2)
    query_full = query.astype(jnp.float32)
    keys_full = lookup_vectors.astype(jnp.float32)
    values_full = values.astype(jnp.float32)
    scores = jnp.einsum('sthd,suhd->shtu', query_full, keys_full)
    causal = positions[:, None] >= positions[None, :]
    gap = cumulative[:, :, :, None] - cumulative[:, :, None, :]
    weights = jnp.where(causal, jnp.exp(jnp.minimum(gap, 0.0)), 0.0)
    probs = (scores * weights).astype(jnp.bfloat16)
    intra = jnp.einsum('shtu,suhd->sthd', probs.astype(jnp.float32), values_full)
    carried = jnp.einsum('sthd,shde->sthe', query_full, old_state, precision=lax.Precision.HIGHEST)
    carried = carried * jnp.exp(cumulative).transpose(0, 2, 1)[:, :, :, None]
    attended = intra + carried
    final_log = cumulative[:, :, length - 1:]
    weighted_keys = keys_full * jnp.exp(final_log - cumulative).transpose(0, 2, 1)[:, :, :, None]
    updated = jnp.exp(final_log)[:, :, :, None] * old_state + jnp.einsum('sthd,sthe->shde', weighted_keys, values_full, precision=lax.Precision.HIGHEST)
    mean_square = lax.optimization_barrier(jnp.mean(attended * attended, axis=-1, keepdims=True))
    normed = attended * lax.rsqrt(mean_square + 1e-05)
    gates = jax.nn.sigmoid(gate_sum).reshape(streams, length, heads, HD)
    hidden = (normed * gates * live_full[:, :, None, None]).astype(jnp.bfloat16).reshape(rows, heads * HD)
    return (hidden, updated)

def reference(tokens, qkv_weight, gate_weight, out_weight, log_decay, states, dest_slot, valid):
    moved = jnp.zeros_like(states).at[dest_slot].set(states)
    blocks = NUM_SEQUENCES // SD
    flat_qkv = qkv_weight.reshape(D, 3 * NUM_ATTENDERS * HD)

    def run(item):
        rows_x, decay_rows, old_state, valid_rows = item
        projected = jnp.dot(rows_x, flat_qkv, preferred_element_type=jnp.float32)
        gate_sum = jnp.dot(rows_x, gate_weight, preferred_element_type=jnp.float32)
        hidden, updated = core(projected, gate_sum, decay_rows, old_state, valid_rows)
        mixed = jnp.dot(hidden, out_weight, preferred_element_type=jnp.float32).astype(jnp.bfloat16)
        return (mixed, updated)
    mixed, updated = lax.map(run, (tokens.reshape(blocks, SD * WINDOW_LENGTH, D), log_decay.reshape(NUM_ATTENDERS, blocks, SD * WINDOW_LENGTH).transpose(1, 0, 2), moved.reshape(blocks, SD, NUM_ATTENDERS, HD, HD), valid.reshape(blocks, SD)))
    return (mixed.reshape(TOKENS, D), updated.reshape(NUM_SEQUENCES, NUM_ATTENDERS, HD, HD))
```

```python
import functools

import jax
import jax.numpy as jnp
from jax import lax
from jax.experimental import pallas as pl
from jax.experimental.pallas import tpu as pltpu
from jax.sharding import PartitionSpec as P

HD = 64
WINDOW_LENGTH = 128
CHUNKS = 3


def move_states(states, dest_slot):
    streams = states.shape[0]
    node_count = lax.axis_size("stream")
    capacity = (streams + node_count - 1) // node_count
    target = dest_slot // streams
    places = dest_slot % streams
    order = jnp.arange(streams, dtype=jnp.int32)
    earlier = (target[None, :] == target[:, None]) & (order[None, :] < order[:, None])
    ranking = jnp.sum(earlier.astype(jnp.int32), axis=1)
    position = target * capacity + ranking
    tail_shape = states.shape[1:]
    outgoing = (
        jnp.zeros((node_count * capacity,) + tail_shape, jnp.float32).at[position].set(states)
    )
    outgoing = outgoing.reshape((node_count, capacity) + tail_shape)
    labels = jnp.full((node_count * capacity,), streams, jnp.int32).at[position].set(places)
    labels = labels.reshape(node_count, capacity)
    incoming, incoming_labels = (
        lax.all_to_all(outgoing, "stream", split_axis=0, concat_axis=0, tiled=True),
        lax.all_to_all(labels, "stream", split_axis=0, concat_axis=0, tiled=True),
    )
    flat_states = incoming.reshape((node_count * capacity,) + tail_shape)
    flat_labels = incoming_labels.reshape(node_count * capacity)
    placed = jnp.zeros((streams + 1,) + tail_shape, jnp.float32).at[flat_labels].set(flat_states)
    return placed[:streams]


MESH = pl.DeviceIdType.MESH


def greet(targets):
    barrier = pltpu.get_barrier_semaphore()
    for target in targets:
        pl.semaphore_signal(barrier, inc=1, device_id=target, device_id_type=MESH)
    pl.semaphore_wait(barrier, len(targets))


def remote(src, dst, send, recv, target):
    return pltpu.make_async_remote_copy(
        src_ref=src, dst_ref=dst, send_sem=send, recv_sem=recv, device_id=target, device_id_type=MESH
    )


def gather_kernel(chips, w_ref, out_ref, send1, recv1, send2, recv2, local):
    me = lax.axis_index("stream")
    tp = lax.axis_index("tp")
    chip, core = me // 2, me % 2
    sibling = (chip * 2 + (1 - core), tp)
    peers = [(((chip + d) % chips) * 2 + core, tp) for d in range(1, chips)]
    greet(peers + [sibling])
    sends = []
    for d in range(1, chips):
        copy = remote(w_ref, out_ref.at[me], send1.at[d], recv1.at[d], peers[d - 1])
        copy.start()
        sends.append(copy)
    copy = remote(w_ref, out_ref.at[me], send2.at[0], recv2.at[0], sibling)
    copy.start()
    sends.append(copy)
    own = pltpu.make_async_copy(w_ref, out_ref.at[me], local)
    own.start()
    for d in range(1, chips):
        source = ((chip - d + chips) % chips) * 2 + core
        slot = out_ref.at[source]
        remote(w_ref, slot, send1.at[d], recv1.at[d], peers[d - 1]).wait_recv()
        copy = remote(slot, slot, send2.at[d], recv2.at[d], sibling)
        copy.start()
        sends.append(copy)
    for d in range(chips):
        source = ((chip - d + chips) % chips) * 2 + (1 - core)
        remote(w_ref, out_ref.at[source], send2.at[d], recv2.at[d], sibling).wait_recv()
    for copy in sends:
        copy.wait_send()
    own.wait()


def gather_rows(weight):
    count = lax.axis_size("stream")
    chips = count // 2
    return pl.pallas_call(
        functools.partial(gather_kernel, chips),
        out_shape=jax.ShapeDtypeStruct((count,) + weight.shape, weight.dtype),
        in_specs=[pl.BlockSpec(memory_space=pl.ANY)],
        out_specs=pl.BlockSpec(memory_space=pl.ANY),
        scratch_shapes=[pltpu.SemaphoreType.DMA((chips,))] * 4 + [pltpu.SemaphoreType.DMA],
        compiler_params=pltpu.CompilerParams(collective_id=0, has_side_effects=True),
        cost_estimate=pl.CostEstimate(flops=0, bytes_accessed=200_000_000, transcendentals=0),
        name="gather_rows",
    )(weight)


def spread_kernel(count, planes, w_ref, out_ref, sendz, recvz, sendx, recvx, sends, recvs, local):
    me = lax.axis_index("stream")
    tp = lax.axis_index("tp")
    chips, per = count // 2, count // planes
    chip, core = me // 2, me % 2
    sibling = (chip * 2 + (1 - core), tp)
    peers = [(((chip + d) % chips) * 2 + core, tp) for d in range(1, chips)]
    column = [(me, (tp + d) % planes) for d in range(1, planes)]
    greet(peers + [sibling] + column)
    owner, place = me // per, me % per
    mine = owner == tp
    own = pltpu.make_async_copy(w_ref, out_ref.at[place, tp], local)
    first = remote(w_ref, out_ref.at[place, tp], sendz, recvz.at[tp], (me, owner))

    @pl.when(mine)
    def _():
        own.start()
        own.wait()
        for d in range(1, planes):
            source = (tp + d) % planes
            remote(w_ref, out_ref.at[place, source], sendz, recvz.at[source], (me, source)).wait_recv()
        for d in range(1, chips):
            remote(out_ref.at[place], out_ref.at[place], sendx.at[d], recvx.at[place // 2], peers[d - 1]).start()

    @pl.when(jnp.logical_not(mine))
    def _():
        first.start()

    for i in range(per // 2):
        slot = out_ref.at[2 * i + core]
        source = tp * per + 2 * i + core

        @pl.when(source != me)
        def _():
            remote(slot, slot, sendx.at[0], recvx.at[i], sibling).wait_recv()

        remote(slot, slot, sends.at[i], recvs.at[i], sibling).start()
    for i in range(per // 2):
        other = out_ref.at[2 * i + (1 - core)]
        remote(other, other, sends.at[i], recvs.at[i], sibling).wait_recv()
    for i in range(per // 2):
        slot = out_ref.at[2 * i + core]
        remote(slot, slot, sends.at[i], recvs.at[i], sibling).wait_send()

    @pl.when(mine)
    def _():
        for d in range(1, chips):
            remote(out_ref.at[place], out_ref.at[place], sendx.at[d], recvx.at[place // 2], peers[d - 1]).wait_send()

    @pl.when(jnp.logical_not(mine))
    def _():
        first.wait_send()


def spread_columns(weight):
    count, planes = lax.axis_size("stream"), lax.axis_size("tp")
    chips, per = count // 2, count // planes
    dma = pltpu.SemaphoreType.DMA
    return pl.pallas_call(
        functools.partial(spread_kernel, count, planes),
        out_shape=jax.ShapeDtypeStruct((per, planes) + weight.shape, weight.dtype),
        in_specs=[pl.BlockSpec(memory_space=pl.ANY)],
        out_specs=pl.BlockSpec(memory_space=pl.ANY),
        scratch_shapes=[dma, dma((planes,)), dma((chips,)), dma((per // 2,)), dma((per // 2,)), dma((per // 2,)), dma],
        compiler_params=pltpu.CompilerParams(collective_id=1, has_side_effects=True),
        cost_estimate=pl.CostEstimate(flops=0, bytes_accessed=200_000_000, transcendentals=0),
        name="spread_columns",
    )(weight)


def attend(qkv_part, gate_part, valid, log_decay, moved):
    streams, heads = moved.shape[:2]
    length = WINDOW_LENGTH
    rows = streams * length
    activated = jax.nn.silu(qkv_part).astype(jnp.bfloat16).reshape(streams, length, 3, heads, HD)
    positions = jnp.arange(length, dtype=jnp.int32)
    live = positions[None, :] < valid[:, None]
    live_half = live.astype(jnp.bfloat16)[:, :, None, None]
    live_full = live.astype(jnp.float32)
    query = activated[:, :, 0]
    lookup_vectors = activated[:, :, 1] * live_half
    values = activated[:, :, 2] * live_half
    decay = log_decay.reshape(heads, streams, length).transpose(1, 0, 2) * live_full[:, None, :]
    lower_ones = (positions[:, None] <= positions[None, :]).astype(jnp.float32)
    cumulative = jnp.einsum("shu,ut->sht", decay, lower_ones, precision=lax.Precision.HIGHEST)
    scores = jnp.einsum(
        "sthd,suhd->shtu", query, lookup_vectors, preferred_element_type=jnp.float32
    )
    causal = positions[:, None] >= positions[None, :]
    gap = cumulative[:, :, :, None] - cumulative[:, :, None, :]
    weights = jnp.where(causal, jnp.exp(jnp.minimum(gap, 0.0)), 0.0)
    probs = (scores * weights).astype(jnp.bfloat16)
    intra = jnp.einsum("shtu,suhd->sthd", probs, values, preferred_element_type=jnp.float32)
    query_full = query.astype(jnp.float32)
    carried = jnp.einsum("sthd,shde->sthe", query_full, moved, precision=lax.Precision.HIGHEST)
    carried = carried * jnp.exp(cumulative).transpose(0, 2, 1)[:, :, :, None]
    attended = intra + carried
    final_log = cumulative[:, :, length - 1 :]
    weighted_keys = (
        lookup_vectors.astype(jnp.float32)
        * jnp.exp(final_log - cumulative).transpose(0, 2, 1)[:, :, :, None]
    )
    updated = jnp.exp(final_log)[:, :, :, None] * moved + jnp.einsum(
        "sthd,sthe->shde",
        weighted_keys,
        values.astype(jnp.float32),
        precision=lax.Precision.HIGHEST,
    )
    mean_square = jnp.mean(attended * attended, axis=-1, keepdims=True)
    normed = attended * lax.rsqrt(mean_square + 1e-05)
    gates = jax.nn.sigmoid(gate_part).reshape(streams, length, heads, HD)
    hidden = (
        (normed * gates * live_full[:, :, None, None])
        .astype(jnp.bfloat16)
        .reshape(rows, heads * HD)
    )
    return hidden, updated


def body(tokens, qkv_weight, gate_weight, out_weight, log_decay, states, dest_slot, valid):
    streams, heads = states.shape[:2]
    width = heads * HD
    chunks = CHUNKS if streams % CHUNKS == 0 else 1
    part = streams // chunks
    rows = part * WINDOW_LENGTH
    features = [
        lax.all_gather(tokens[c * rows : (c + 1) * rows], "tp", axis=1, tiled=True)
        for c in range(chunks)
    ]
    local = jnp.concatenate([qkv_weight.reshape(-1, 3 * width), gate_weight], axis=1)
    moved = move_states(states, dest_slot)
    weights = gather_rows(local)
    weights = weights.reshape(-1, 4 * width)
    gathered, updates = [], []
    for c in range(chunks):
        projected = jnp.dot(features[c], weights, preferred_element_type=jnp.float32)
        hidden, updated = attend(
            projected[:, : 3 * width],
            projected[:, 3 * width :],
            valid[c * part : (c + 1) * part],
            log_decay[:, c * rows : (c + 1) * rows],
            moved[c * part : (c + 1) * part],
        )
        gathered.append(lax.all_gather(hidden, "tp", axis=1, tiled=True))
        updates.append(updated)
    out_weight, _ = lax.optimization_barrier((out_weight, hidden))
    spread = spread_columns(out_weight)
    per = spread.shape[0]
    full_rows = spread.reshape(per, -1, out_weight.shape[1]).transpose(1, 0, 2)
    full_rows = full_rows.reshape(full_rows.shape[0], -1)
    mixed = [
        jnp.dot(part_heads, full_rows, preferred_element_type=jnp.float32).astype(jnp.bfloat16)
        for part_heads in gathered
    ]
    return (jnp.concatenate(mixed, axis=0), jnp.concatenate(updates, axis=0))


def solution(mesh):
    return jax.shard_map(
        body,
        mesh=mesh,
        in_specs=(
            P("stream", "tp"),
            P("stream", None, "tp"),
            P("stream", "tp"),
            P("tp", "stream"),
            P("tp", "stream"),
            P("stream", "tp", None, None),
            P("stream"),
            P("stream"),
        ),
        out_specs=(P("stream", "tp"), P("stream", "tp", None, None)),
        check_vma=False,
    )
```

```python
import functools

import jax
import jax.numpy as jnp
from jax import lax
from jax.experimental import pallas as pl
from jax.experimental.pallas import tpu as pltpu
from jax.sharding import PartitionSpec as P

HD = 64
WINDOW_LENGTH = 128
CHUNKS = 2


def move_states(states, dest_slot):
    streams = states.shape[0]
    node_count = lax.axis_size("stream")
    capacity = (streams + node_count - 1) // node_count
    target = dest_slot // streams
    places = dest_slot % streams
    order = jnp.arange(streams, dtype=jnp.int32)
    earlier = (target[None, :] == target[:, None]) & (order[None, :] < order[:, None])
    ranking = jnp.sum(earlier.astype(jnp.int32), axis=1)
    position = target * capacity + ranking
    tail_shape = states.shape[1:]
    outgoing = (
        jnp.zeros((node_count * capacity,) + tail_shape, jnp.float32).at[position].set(states)
    )
    outgoing = outgoing.reshape((node_count, capacity) + tail_shape)
    labels = jnp.full((node_count * capacity,), streams, jnp.int32).at[position].set(places)
    labels = labels.reshape(node_count, capacity)
    incoming, incoming_labels = (
        lax.all_to_all(outgoing, "stream", split_axis=0, concat_axis=0, tiled=True),
        lax.all_to_all(labels, "stream", split_axis=0, concat_axis=0, tiled=True),
    )
    flat_states = incoming.reshape((node_count * capacity,) + tail_shape)
    flat_labels = incoming_labels.reshape(node_count * capacity)
    placed = jnp.zeros((streams + 1,) + tail_shape, jnp.float32).at[flat_labels].set(flat_states)
    return placed[:streams]


MESH = pl.DeviceIdType.MESH


def greet(targets):
    barrier = pltpu.get_barrier_semaphore()
    for target in targets:
        pl.semaphore_signal(barrier, inc=1, device_id=target, device_id_type=MESH)
    pl.semaphore_wait(barrier, len(targets))


def remote(src, dst, send, recv, target):
    return pltpu.make_async_remote_copy(
        src_ref=src, dst_ref=dst, send_sem=send, recv_sem=recv, device_id=target, device_id_type=MESH
    )


def gather_kernel(chips, planes, w_ref, o_ref, out_ref, col_ref, send1, recv1, send2, recv2, sendz, recvz, local):
    me = lax.axis_index("stream")
    tp = lax.axis_index("tp")
    chip, core = me // 2, me % 2
    per = chips * 2 // planes
    owner = me // per
    mine = owner == tp
    sibling = (chip * 2 + (1 - core), tp)
    peers = [(((chip + d) % chips) * 2 + core, tp) for d in range(1, chips)]
    column = [(me, (tp + d) % planes) for d in range(1, planes)]
    greet(peers + [sibling] + column)
    sends = []
    for d in range(1, chips):
        copy = remote(w_ref, out_ref.at[me], send1.at[d], recv1.at[d], peers[d - 1])
        copy.start()
        sends.append(copy)
    copy = remote(w_ref, out_ref.at[me], send2.at[0], recv2.at[0], sibling)
    copy.start()
    sends.append(copy)
    hop = remote(o_ref, col_ref.at[tp], sendz, recvz.at[tp], (me, owner))

    @pl.when(jnp.logical_not(mine))
    def _():
        hop.start()

    own = pltpu.make_async_copy(w_ref, out_ref.at[me], local.at[0])
    own.start()
    kept = pltpu.make_async_copy(o_ref, col_ref.at[tp], local.at[1])
    kept.start()
    for d in range(1, chips):
        source = ((chip - d + chips) % chips) * 2 + core
        slot = out_ref.at[source]
        remote(w_ref, slot, send1.at[d], recv1.at[d], peers[d - 1]).wait_recv()
        copy = remote(slot, slot, send2.at[d], recv2.at[d], sibling)
        copy.start()
        sends.append(copy)
    for d in range(chips):
        source = ((chip - d + chips) % chips) * 2 + (1 - core)
        remote(w_ref, out_ref.at[source], send2.at[d], recv2.at[d], sibling).wait_recv()

    @pl.when(mine)
    def _():
        for d in range(1, planes):
            source = (tp + d) % planes
            remote(o_ref, col_ref.at[source], sendz, recvz.at[source], (me, source)).wait_recv()

    @pl.when(jnp.logical_not(mine))
    def _():
        hop.wait_send()

    for copy in sends:
        copy.wait_send()
    own.wait()
    kept.wait()


def gather_rows(weight, out_weight):
    count, planes = lax.axis_size("stream"), lax.axis_size("tp")
    chips = count // 2
    dma = pltpu.SemaphoreType.DMA
    anywhere = pl.BlockSpec(memory_space=pl.ANY)
    return pl.pallas_call(
        functools.partial(gather_kernel, chips, planes),
        out_shape=(
            jax.ShapeDtypeStruct((count,) + weight.shape, weight.dtype),
            jax.ShapeDtypeStruct((planes,) + out_weight.shape, out_weight.dtype),
        ),
        in_specs=[anywhere, anywhere],
        out_specs=(anywhere, anywhere),
        scratch_shapes=[dma((chips,))] * 4 + [dma, dma((planes,)), dma((2,))],
        compiler_params=pltpu.CompilerParams(collective_id=0, has_side_effects=True),
        cost_estimate=pl.CostEstimate(flops=0, bytes_accessed=200_000_000, transcendentals=0),
        name="gather_rows",
    )(weight, out_weight)


def spread_kernel(count, planes, col_ref, out_ref, sendx, recvx, sends, recvs, local):
    me = lax.axis_index("stream")
    tp = lax.axis_index("tp")
    chips, per = count // 2, count // planes
    chip, core = me // 2, me % 2
    sibling = (chip * 2 + (1 - core), tp)
    peers = [(((chip + d) % chips) * 2 + core, tp) for d in range(1, chips)]
    greet(peers + [sibling])
    owner, place = me // per, me % per
    mine = owner == tp

    @pl.when(mine)
    def _():
        for d in range(1, chips):
            remote(col_ref, out_ref.at[place], sendx.at[d], recvx.at[place // 2], peers[d - 1]).start()
        own = pltpu.make_async_copy(col_ref, out_ref.at[place], local)
        own.start()
        own.wait()

    for i in range(per // 2):
        slot = out_ref.at[2 * i + core]
        source = tp * per + 2 * i + core

        @pl.when(source != me)
        def _():
            remote(slot, slot, sendx.at[0], recvx.at[i], sibling).wait_recv()

        remote(slot, slot, sends.at[i], recvs.at[i], sibling).start()
    for i in range(per // 2):
        other = out_ref.at[2 * i + (1 - core)]
        remote(other, other, sends.at[i], recvs.at[i], sibling).wait_recv()
    for i in range(per // 2):
        slot = out_ref.at[2 * i + core]
        remote(slot, slot, sends.at[i], recvs.at[i], sibling).wait_send()

    @pl.when(mine)
    def _():
        for d in range(1, chips):
            remote(col_ref, out_ref.at[place], sendx.at[d], recvx.at[place // 2], peers[d - 1]).wait_send()


def spread_columns(columns):
    count, planes = lax.axis_size("stream"), lax.axis_size("tp")
    chips, per = count // 2, count // planes
    dma = pltpu.SemaphoreType.DMA
    return pl.pallas_call(
        functools.partial(spread_kernel, count, planes),
        out_shape=jax.ShapeDtypeStruct((per,) + columns.shape, columns.dtype),
        in_specs=[pl.BlockSpec(memory_space=pl.ANY)],
        out_specs=pl.BlockSpec(memory_space=pl.ANY),
        scratch_shapes=[dma((chips,)), dma((per // 2,)), dma((per // 2,)), dma((per // 2,)), dma],
        compiler_params=pltpu.CompilerParams(collective_id=1, has_side_effects=True),
        cost_estimate=pl.CostEstimate(flops=0, bytes_accessed=200_000_000, transcendentals=0),
        name="spread_columns",
    )(columns)


def halves(x):
    high = x.astype(jnp.bfloat16)
    return high, (x - high.astype(jnp.float32)).astype(jnp.bfloat16)


def product(a, b, left, right):
    return lax.dot_general(a, b, (((left,), (right,)), ((), ())), preferred_element_type=jnp.float32)


def attend_kernel(first, heads, valid_ref, proj_ref, decay_ref, moved_ref, *refs):
    hidden_ref, updated_ref = refs[-2:]
    length, width = WINDOW_LENGTH, heads * HD
    count = valid_ref[first + pl.program_id(0)]
    column = lax.broadcasted_iota(jnp.int32, (length, 1), 0)
    live = (column < count).astype(jnp.float32)
    rows = lax.broadcasted_iota(jnp.int32, (length, length), 0)
    cols = lax.broadcasted_iota(jnp.int32, (length, length), 1)
    live_row = lax.broadcasted_iota(jnp.int32, (heads, length), 1) < count
    decay = jnp.where(live_row, decay_ref[...], 0.0)
    ones = (rows <= cols).astype(jnp.float32)
    across = lax.dot_general(
        decay,
        ones,
        (((1,), (0,)), ((), ())),
        precision=lax.Precision.HIGHEST,
        preferred_element_type=jnp.float32,
    )
    down = across.T
    causal = rows >= cols
    for pair in range(heads // 2):
        block = slice(pair * 2 * HD, (pair + 1) * 2 * HD)

        def active(part):
            x = proj_ref[:, part * width + block.start : part * width + block.stop]
            return x * jax.nn.sigmoid(x)

        queries = active(0).astype(jnp.bfloat16)
        keys = (active(1) * live).astype(jnp.bfloat16)
        values = (active(2) * live).astype(jnp.bfloat16)
        gates = jax.nn.sigmoid(proj_ref[:, 3 * width + block.start : 3 * width + block.stop]) * live
        outs = []
        for side in range(2):
            h = 2 * pair + side
            lanes = slice(side * HD, (side + 1) * HD)
            q, k, v = queries[:, lanes], keys[:, lanes], values[:, lanes]
            along, above = down[:, h : h + 1], across[h : h + 1, :]
            last = across[h : h + 1, length - 1 :]
            weights = jnp.where(causal, jnp.exp(jnp.minimum(along - above, 0.0)), 0.0)
            probs = (product(q, k, 1, 1) * weights).astype(jnp.bfloat16)
            old = moved_ref[0, h]
            high, low = halves(old)
            carried = product(q, high, 1, 0) + product(q, low, 1, 0)
            attended = product(probs, v, 1, 0) + carried * jnp.exp(along)
            high, low = halves(k.astype(jnp.float32) * jnp.exp(last - along))
            updated_ref[0, h] = jnp.exp(last) * old + (product(high, v, 0, 0) + product(low, v, 0, 0))
            mean_square = jnp.mean(attended * attended, axis=1, keepdims=True)
            outs.append(attended * lax.rsqrt(mean_square + 1e-05))
        hidden_ref[:, block] = (jnp.concatenate(outs, axis=1) * gates).astype(jnp.bfloat16)


def attend(projected, valid, log_decay, moved, first, part, earlier):
    streams, heads = moved.shape[:2]
    length, width = WINDOW_LENGTH, heads * HD
    in_specs = [
        pl.BlockSpec((length, 4 * width), lambda i, v: (i, 0)),
        pl.BlockSpec((heads, length), lambda i, v: (0, first + i)),
        pl.BlockSpec((1, heads, HD, HD), lambda i, v: (first + i, 0, 0, 0)),
    ]
    operands = [projected, log_decay, moved]
    aliases = {}
    if earlier is not None:
        in_specs.append(pl.BlockSpec(memory_space=pl.ANY))
        operands.append(earlier)
        aliases = {4: 1}
    return pl.pallas_call(
        functools.partial(attend_kernel, first, heads),
        out_shape=(
            jax.ShapeDtypeStruct((part * length, width), jnp.bfloat16),
            jax.ShapeDtypeStruct(moved.shape, jnp.float32),
        ),
        grid_spec=pltpu.PrefetchScalarGridSpec(
            num_scalar_prefetch=1,
            grid=(part,),
            in_specs=in_specs,
            out_specs=(
                pl.BlockSpec((length, width), lambda i, v: (i, 0)),
                pl.BlockSpec((1, heads, HD, HD), lambda i, v: (first + i, 0, 0, 0)),
            ),
        ),
        input_output_aliases=aliases,
        cost_estimate=pl.CostEstimate(flops=0, bytes_accessed=40_000_000, transcendentals=0),
        name="attend",
    )(valid, *operands)


def body(tokens, qkv_weight, gate_weight, out_weight, log_decay, states, dest_slot, valid):
    streams, heads = states.shape[:2]
    width = heads * HD
    chunks = CHUNKS if streams % CHUNKS == 0 else 1
    part = streams // chunks
    rows = part * WINDOW_LENGTH
    features = [
        lax.all_gather(tokens[c * rows : (c + 1) * rows], "tp", axis=1, tiled=True)
        for c in range(chunks)
    ]
    local = jnp.concatenate([qkv_weight.reshape(-1, 3 * width), gate_weight], axis=1)
    moved = move_states(states, dest_slot)
    weights, columns = gather_rows(local, out_weight)
    weights = weights.reshape(-1, 4 * width)
    gathered, updated = [], None
    for c in range(chunks):
        projected = jnp.dot(features[c], weights, preferred_element_type=jnp.float32)
        hidden, updated = attend(projected, valid, log_decay, moved, c * part, part, updated)
        gathered.append(lax.all_gather(hidden, "tp", axis=1, tiled=True))
    columns, _ = lax.optimization_barrier((columns, hidden))
    spread = spread_columns(columns)
    per = spread.shape[0]
    full_rows = spread.reshape(per, -1, out_weight.shape[1]).transpose(1, 0, 2)
    full_rows = full_rows.reshape(full_rows.shape[0], -1)
    mixed = [
        jnp.dot(part_heads, full_rows, preferred_element_type=jnp.float32).astype(jnp.bfloat16)
        for part_heads in gathered
    ]
    return (jnp.concatenate(mixed, axis=0), updated)


def solution(mesh):
    return jax.shard_map(
        body,
        mesh=mesh,
        in_specs=(
            P("stream", "tp"),
            P("stream", None, "tp"),
            P("stream", "tp"),
            P("tp", "stream"),
            P("tp", "stream"),
            P("stream", "tp", None, None),
            P("stream"),
            P("stream"),
        ),
        out_specs=(P("stream", "tp"), P("stream", "tp", None, None)),
        check_vma=False,
    )
```

```python
import functools

import jax
import jax.numpy as jnp
from jax import lax
from jax.experimental import pallas as pl
from jax.experimental.pallas import tpu as pltpu
from jax.sharding import PartitionSpec as P

HD = 64
WINDOW_LENGTH = 128


def move_states(states, dest_slot):
    streams = states.shape[0]
    node_count = lax.axis_size("stream")
    capacity = (streams + node_count - 1) // node_count
    target = dest_slot // streams
    places = dest_slot % streams
    order = jnp.arange(streams, dtype=jnp.int32)
    earlier = (target[None, :] == target[:, None]) & (order[None, :] < order[:, None])
    ranking = jnp.sum(earlier.astype(jnp.int32), axis=1)
    position = target * capacity + ranking
    tail_shape = states.shape[1:]
    outgoing = (
        jnp.zeros((node_count * capacity,) + tail_shape, jnp.float32).at[position].set(states)
    )
    outgoing = outgoing.reshape((node_count, capacity) + tail_shape)
    labels = jnp.full((node_count * capacity,), streams, jnp.int32).at[position].set(places)
    labels = labels.reshape(node_count, capacity)
    incoming, incoming_labels = (
        lax.all_to_all(outgoing, "stream", split_axis=0, concat_axis=0, tiled=True),
        lax.all_to_all(labels, "stream", split_axis=0, concat_axis=0, tiled=True),
    )
    flat_states = incoming.reshape((node_count * capacity,) + tail_shape)
    flat_labels = incoming_labels.reshape(node_count * capacity)
    placed = jnp.zeros((streams + 1,) + tail_shape, jnp.float32).at[flat_labels].set(flat_states)
    return placed[:streams]


MESH = pl.DeviceIdType.MESH


def greet(targets):
    barrier = pltpu.get_barrier_semaphore()
    for target in targets:
        pl.semaphore_signal(barrier, inc=1, device_id=target, device_id_type=MESH)
    pl.semaphore_wait(barrier, len(targets))


def remote(src, dst, send, recv, target):
    return pltpu.make_async_remote_copy(
        src_ref=src, dst_ref=dst, send_sem=send, recv_sem=recv, device_id=target, device_id_type=MESH
    )


def line_copies(planes, source_ref, all_ref, send, recv, local):
    me = lax.axis_index("stream")
    tp = lax.axis_index("tp")
    wide = source_ref.shape[1]

    def place(plane):
        return all_ref.at[:, pl.ds(pl.multiple_of(plane * wide, wide), wide)]

    out, back = [], []
    for d in range(1, planes):
        target = (me, (tp + d) % planes)
        out.append(remote(source_ref, place(tp), send.at[d], recv.at[d], target))
        source = (tp - d + planes) % planes
        back.append(remote(source_ref, place(source), send.at[d], recv.at[d], target))
    own = pltpu.make_async_copy(source_ref, place(tp), local)

    def start():
        for copy in out:
            copy.start()
        own.start()

    def wait():
        for copy in back:
            copy.wait_recv()
        for copy in out:
            copy.wait_send()
        own.wait()

    return start, wait


def gather_kernel(
    chips,
    planes,
    rows,
    w_ref,
    o_ref,
    t_ref,
    out_ref,
    col_ref,
    feature_ref,
    send1,
    recv1,
    send2,
    recv2,
    sendz,
    recvz,
    sendt,
    recvt,
    local,
):
    me = lax.axis_index("stream")
    tp = lax.axis_index("tp")
    chip, core = me // 2, me % 2
    per = chips * 2 // planes
    owner = me // per
    mine = owner == tp
    sibling = (chip * 2 + (1 - core), tp)
    peers = [(((chip + d) % chips) * 2 + core, tp) for d in range(1, chips)]
    column = [(me, (tp + d) % planes) for d in range(1, planes)]
    greet(peers + [sibling] + column)
    sends = []
    for d in range(1, chips):
        copy = remote(w_ref, out_ref.at[me], send1.at[d], recv1.at[d], peers[d - 1])
        copy.start()
        sends.append(copy)
    copy = remote(w_ref, out_ref.at[me], send2.at[0], recv2.at[0], sibling)
    copy.start()
    sends.append(copy)
    start_line, wait_line = line_copies(
        planes, t_ref.at[pl.ds(0, rows)], feature_ref, sendt, recvt, local.at[2]
    )
    start_line()
    hop = remote(o_ref, col_ref.at[tp], sendz, recvz.at[tp], (me, owner))

    @pl.when(jnp.logical_not(mine))
    def _():
        hop.start()

    own = pltpu.make_async_copy(w_ref, out_ref.at[me], local.at[0])
    own.start()
    kept = pltpu.make_async_copy(o_ref, col_ref.at[tp], local.at[1])
    kept.start()
    for d in range(1, chips):
        source = ((chip - d + chips) % chips) * 2 + core
        slot = out_ref.at[source]
        remote(w_ref, slot, send1.at[d], recv1.at[d], peers[d - 1]).wait_recv()
        copy = remote(slot, slot, send2.at[d], recv2.at[d], sibling)
        copy.start()
        sends.append(copy)
    for d in range(chips):
        source = ((chip - d + chips) % chips) * 2 + (1 - core)
        remote(w_ref, out_ref.at[source], send2.at[d], recv2.at[d], sibling).wait_recv()

    @pl.when(mine)
    def _():
        for d in range(1, planes):
            source = (tp + d) % planes
            remote(o_ref, col_ref.at[source], sendz, recvz.at[source], (me, source)).wait_recv()

    @pl.when(jnp.logical_not(mine))
    def _():
        hop.wait_send()

    wait_line()
    for copy in sends:
        copy.wait_send()
    own.wait()
    kept.wait()


def gather_rows(weight, out_weight, tokens, rows):
    count, planes = lax.axis_size("stream"), lax.axis_size("tp")
    chips = count // 2
    dma = pltpu.SemaphoreType.DMA
    anywhere = pl.BlockSpec(memory_space=pl.ANY)
    return pl.pallas_call(
        functools.partial(gather_kernel, chips, planes, rows),
        out_shape=(
            jax.ShapeDtypeStruct((count,) + weight.shape, weight.dtype),
            jax.ShapeDtypeStruct((planes,) + out_weight.shape, out_weight.dtype),
            jax.ShapeDtypeStruct((rows, planes * tokens.shape[1]), tokens.dtype),
        ),
        in_specs=[anywhere] * 3,
        out_specs=(anywhere,) * 3,
        scratch_shapes=[dma((chips,))] * 4 + [dma] + [dma((planes,))] * 3 + [dma((3,))],
        compiler_params=pltpu.CompilerParams(collective_id=0, has_side_effects=True),
        cost_estimate=pl.CostEstimate(flops=0, bytes_accessed=200_000_000, transcendentals=0),
        name="gather_rows",
    )(weight, out_weight, tokens)


def spread_kernel(
    count, planes, col_ref, h_ref, out_ref, heads_ref, sendx, recvx, sends, recvs, sendh, recvh, local
):
    me = lax.axis_index("stream")
    tp = lax.axis_index("tp")
    chips, per = count // 2, count // planes
    chip, core = me // 2, me % 2
    sibling = (chip * 2 + (1 - core), tp)
    peers = [(((chip + d) % chips) * 2 + core, tp) for d in range(1, chips)]
    column = [(me, (tp + d) % planes) for d in range(1, planes)]
    greet(peers + [sibling] + column)
    owner, place = me // per, me % per
    start_line, wait_line = line_copies(planes, h_ref, heads_ref, sendh, recvh, local.at[1])
    start_line()
    mine = owner == tp

    @pl.when(mine)
    def _():
        for d in range(1, chips):
            remote(col_ref, out_ref.at[place], sendx.at[d], recvx.at[place // 2], peers[d - 1]).start()
        own = pltpu.make_async_copy(col_ref, out_ref.at[place], local.at[0])
        own.start()
        own.wait()

    for i in range(per // 2):
        slot = out_ref.at[2 * i + core]
        source = tp * per + 2 * i + core

        @pl.when(source != me)
        def _():
            remote(slot, slot, sendx.at[0], recvx.at[i], sibling).wait_recv()

        remote(slot, slot, sends.at[i], recvs.at[i], sibling).start()
    for i in range(per // 2):
        other = out_ref.at[2 * i + (1 - core)]
        remote(other, other, sends.at[i], recvs.at[i], sibling).wait_recv()
    for i in range(per // 2):
        slot = out_ref.at[2 * i + core]
        remote(slot, slot, sends.at[i], recvs.at[i], sibling).wait_send()

    @pl.when(mine)
    def _():
        for d in range(1, chips):
            remote(col_ref, out_ref.at[place], sendx.at[d], recvx.at[place // 2], peers[d - 1]).wait_send()

    wait_line()


def spread_columns(columns, hidden):
    count, planes = lax.axis_size("stream"), lax.axis_size("tp")
    chips, per = count // 2, count // planes
    dma = pltpu.SemaphoreType.DMA
    return pl.pallas_call(
        functools.partial(spread_kernel, count, planes),
        out_shape=(
            jax.ShapeDtypeStruct((per,) + columns.shape, columns.dtype),
            jax.ShapeDtypeStruct((hidden.shape[0], planes * hidden.shape[1]), hidden.dtype),
        ),
        in_specs=[pl.BlockSpec(memory_space=pl.ANY)] * 2,
        out_specs=(pl.BlockSpec(memory_space=pl.ANY),) * 2,
        scratch_shapes=[dma((chips,))] + [dma((per // 2,))] * 3 + [dma((planes,))] * 2 + [dma((2,))],
        compiler_params=pltpu.CompilerParams(collective_id=1, has_side_effects=True),
        cost_estimate=pl.CostEstimate(flops=0, bytes_accessed=200_000_000, transcendentals=0),
        name="spread_columns",
    )(columns, hidden)


def halves(x):
    high = x.astype(jnp.bfloat16)
    return high, (x - high.astype(jnp.float32)).astype(jnp.bfloat16)


def product(a, b, left, right):
    return lax.dot_general(a, b, (((left,), (right,)), ((), ())), preferred_element_type=jnp.float32)


def attend_kernel(first, heads, valid_ref, proj_ref, decay_ref, moved_ref, *refs):
    hidden_ref, updated_ref = refs[-2:]
    length, width = WINDOW_LENGTH, heads * HD
    count = valid_ref[first + pl.program_id(0)]
    column = lax.broadcasted_iota(jnp.int32, (length, 1), 0)
    live = (column < count).astype(jnp.float32)
    rows = lax.broadcasted_iota(jnp.int32, (length, length), 0)
    cols = lax.broadcasted_iota(jnp.int32, (length, length), 1)
    live_row = lax.broadcasted_iota(jnp.int32, (heads, length), 1) < count
    decay = jnp.where(live_row, decay_ref[...], 0.0)
    ones = (rows <= cols).astype(jnp.float32)
    across = lax.dot_general(
        decay,
        ones,
        (((1,), (0,)), ((), ())),
        precision=lax.Precision.HIGHEST,
        preferred_element_type=jnp.float32,
    )
    down = across.T
    causal = rows >= cols
    for pair in range(heads // 2):
        block = slice(pair * 2 * HD, (pair + 1) * 2 * HD)

        def active(part):
            x = proj_ref[:, part * width + block.start : part * width + block.stop]
            return x * jax.nn.sigmoid(x)

        queries = active(0).astype(jnp.bfloat16)
        keys = (active(1) * live).astype(jnp.bfloat16)
        values = (active(2) * live).astype(jnp.bfloat16)
        gates = jax.nn.sigmoid(proj_ref[:, 3 * width + block.start : 3 * width + block.stop]) * live
        outs = []
        for side in range(2):
            h = 2 * pair + side
            lanes = slice(side * HD, (side + 1) * HD)
            q, k, v = queries[:, lanes], keys[:, lanes], values[:, lanes]
            along, above = down[:, h : h + 1], across[h : h + 1, :]
            last = across[h : h + 1, length - 1 :]
            weights = jnp.where(causal, jnp.exp(jnp.minimum(along - above, 0.0)), 0.0)
            probs = (product(q, k, 1, 1) * weights).astype(jnp.bfloat16)
            old = moved_ref[0, h]
            high, low = halves(old)
            carried = product(q, high, 1, 0) + product(q, low, 1, 0)
            attended = product(probs, v, 1, 0) + carried * jnp.exp(along)
            high, low = halves(k.astype(jnp.float32) * jnp.exp(last - along))
            updated_ref[0, h] = jnp.exp(last) * old + (product(high, v, 0, 0) + product(low, v, 0, 0))
            mean_square = jnp.mean(attended * attended, axis=1, keepdims=True)
            outs.append(attended * lax.rsqrt(mean_square + 1e-05))
        hidden_ref[:, block] = (jnp.concatenate(outs, axis=1) * gates).astype(jnp.bfloat16)


def attend(projected, valid, log_decay, moved, first, part, earlier):
    streams, heads = moved.shape[:2]
    length, width = WINDOW_LENGTH, heads * HD
    in_specs = [
        pl.BlockSpec((length, 4 * width), lambda i, v: (i, 0)),
        pl.BlockSpec((heads, length), lambda i, v: (0, first + i)),
        pl.BlockSpec((1, heads, HD, HD), lambda i, v: (first + i, 0, 0, 0)),
    ]
    operands = [projected, log_decay, moved]
    aliases = {}
    if earlier is not None:
        in_specs.append(pl.BlockSpec(memory_space=pl.ANY))
        operands.append(earlier)
        aliases = {4: 1}
    return pl.pallas_call(
        functools.partial(attend_kernel, first, heads),
        out_shape=(
            jax.ShapeDtypeStruct((part * length, width), jnp.bfloat16),
            jax.ShapeDtypeStruct(moved.shape, jnp.float32),
        ),
        grid_spec=pltpu.PrefetchScalarGridSpec(
            num_scalar_prefetch=1,
            grid=(part,),
            in_specs=in_specs,
            out_specs=(
                pl.BlockSpec((length, width), lambda i, v: (i, 0)),
                pl.BlockSpec((1, heads, HD, HD), lambda i, v: (first + i, 0, 0, 0)),
            ),
        ),
        input_output_aliases=aliases,
        cost_estimate=pl.CostEstimate(flops=0, bytes_accessed=40_000_000, transcendentals=0),
        name="attend",
    )(valid, *operands)


def body(tokens, qkv_weight, gate_weight, out_weight, log_decay, states, dest_slot, valid):
    streams, heads = states.shape[:2]
    width = heads * HD
    lead, tail = streams // 6, streams // 3
    middle = (streams - lead - tail) // 2
    parts = [lead, middle, streams - lead - tail - middle, tail]
    firsts = [sum(parts[:c]) for c in range(len(parts))]
    features = [None]
    for first, part in zip(firsts[1:], parts[1:]):
        piece = tokens[first * WINDOW_LENGTH : (first + part) * WINDOW_LENGTH]
        features.append(lax.all_gather(piece, "tp", axis=1, tiled=True))
    local = jnp.concatenate([qkv_weight.reshape(-1, 3 * width), gate_weight], axis=1)
    moved = move_states(states, dest_slot)
    weights, columns, features[0] = gather_rows(local, out_weight, tokens, lead * WINDOW_LENGTH)
    weights = weights.reshape(-1, 4 * width)
    gathered, updated = [], None
    for c, part in enumerate(parts):
        projected = jnp.dot(features[c], weights, preferred_element_type=jnp.float32)
        hidden, updated = attend(projected, valid, log_decay, moved, firsts[c], part, updated)
        if c + 1 < len(parts):
            gathered.append(lax.all_gather(hidden, "tp", axis=1, tiled=True))
    spread, heads_last = spread_columns(columns, hidden)
    gathered.append(heads_last)
    per = spread.shape[0]
    full_rows = spread.reshape(per, -1, out_weight.shape[1]).transpose(1, 0, 2)
    full_rows = full_rows.reshape(full_rows.shape[0], -1)
    mixed = [
        jnp.dot(part_heads, full_rows, preferred_element_type=jnp.float32).astype(jnp.bfloat16)
        for part_heads in gathered
    ]
    return (jnp.concatenate(mixed, axis=0), updated)


def solution(mesh):
    return jax.shard_map(
        body,
        mesh=mesh,
        in_specs=(
            P("stream", "tp"),
            P("stream", None, "tp"),
            P("stream", "tp"),
            P("tp", "stream"),
            P("tp", "stream"),
            P("stream", "tp", None, None),
            P("stream"),
            P("stream"),
        ),
        out_specs=(P("stream", "tp"), P("stream", "tp", None, None)),
        check_vma=False,
    )
```

```python
import functools

import jax
import jax.numpy as jnp
from jax import lax
from jax.experimental import pallas as pl
from jax.experimental.pallas import tpu as pltpu
from jax.sharding import PartitionSpec as P

HD = 64
WINDOW_LENGTH = 128


def move_states(states, dest_slot):
    streams = states.shape[0]
    node_count = lax.axis_size("stream")
    capacity = (streams + node_count - 1) // node_count
    target = dest_slot // streams
    places = dest_slot % streams
    order = jnp.arange(streams, dtype=jnp.int32)
    earlier = (target[None, :] == target[:, None]) & (order[None, :] < order[:, None])
    ranking = jnp.sum(earlier.astype(jnp.int32), axis=1)
    position = target * capacity + ranking
    tail_shape = states.shape[1:]
    outgoing = (
        jnp.zeros((node_count * capacity,) + tail_shape, jnp.float32).at[position].set(states)
    )
    outgoing = outgoing.reshape((node_count, capacity) + tail_shape)
    labels = jnp.full((node_count * capacity,), streams, jnp.int32).at[position].set(places)
    labels = labels.reshape(node_count, capacity)
    incoming, incoming_labels = (
        lax.all_to_all(outgoing, "stream", split_axis=0, concat_axis=0, tiled=True),
        lax.all_to_all(labels, "stream", split_axis=0, concat_axis=0, tiled=True),
    )
    flat_states = incoming.reshape((node_count * capacity,) + tail_shape)
    flat_labels = incoming_labels.reshape(node_count * capacity)
    placed = jnp.zeros((streams + 1,) + tail_shape, jnp.float32).at[flat_labels].set(flat_states)
    return placed[:streams]


MESH = pl.DeviceIdType.MESH


def greet(targets):
    barrier = pltpu.get_barrier_semaphore()
    for target in targets:
        pl.semaphore_signal(barrier, inc=1, device_id=target, device_id_type=MESH)
    pl.semaphore_wait(barrier, len(targets))


def remote(src, dst, send, recv, target):
    return pltpu.make_async_remote_copy(
        src_ref=src, dst_ref=dst, send_sem=send, recv_sem=recv, device_id=target, device_id_type=MESH
    )


def line_copies(planes, source_ref, all_ref, send, recv, local):
    me = lax.axis_index("stream")
    tp = lax.axis_index("tp")
    wide = source_ref.shape[1]

    def place(plane):
        return all_ref.at[:, pl.ds(pl.multiple_of(plane * wide, wide), wide)]

    out, back = [], []
    for d in range(1, planes):
        target = (me, (tp + d) % planes)
        out.append(remote(source_ref, place(tp), send.at[d], recv.at[d], target))
        source = (tp - d + planes) % planes
        back.append(remote(source_ref, place(source), send.at[d], recv.at[d], target))
    own = pltpu.make_async_copy(source_ref, place(tp), local)

    def start():
        for copy in out:
            copy.start()
        own.start()

    def wait():
        for copy in back:
            copy.wait_recv()
        for copy in out:
            copy.wait_send()
        own.wait()

    return start, wait


def gather_kernel(
    chips,
    planes,
    rows,
    w_ref,
    o_ref,
    t_ref,
    out_ref,
    col_ref,
    feature_ref,
    send1,
    recv1,
    send2,
    recv2,
    sendz,
    recvz,
    sendt,
    recvt,
    local,
):
    me = lax.axis_index("stream")
    tp = lax.axis_index("tp")
    chip, core = me // 2, me % 2
    per = chips * 2 // planes
    owner = me // per
    mine = owner == tp
    sibling = (chip * 2 + (1 - core), tp)
    peers = [(((chip + d) % chips) * 2 + core, tp) for d in range(1, chips)]
    column = [(me, (tp + d) % planes) for d in range(1, planes)]
    greet(peers + [sibling] + column)
    sends = []
    for d in range(1, chips):
        copy = remote(w_ref, out_ref.at[me], send1.at[d], recv1.at[d], peers[d - 1])
        copy.start()
        sends.append(copy)
    copy = remote(w_ref, out_ref.at[me], send2.at[0], recv2.at[0], sibling)
    copy.start()
    sends.append(copy)
    start_line, wait_line = line_copies(
        planes, t_ref.at[pl.ds(0, rows)], feature_ref, sendt, recvt, local.at[2]
    )
    start_line()
    hop = remote(o_ref, col_ref.at[tp], sendz, recvz.at[tp], (me, owner))

    @pl.when(jnp.logical_not(mine))
    def _():
        hop.start()

    own = pltpu.make_async_copy(w_ref, out_ref.at[me], local.at[0])
    own.start()
    kept = pltpu.make_async_copy(o_ref, col_ref.at[tp], local.at[1])
    kept.start()
    for d in range(1, chips):
        source = ((chip - d + chips) % chips) * 2 + core
        slot = out_ref.at[source]
        remote(w_ref, slot, send1.at[d], recv1.at[d], peers[d - 1]).wait_recv()
        copy = remote(slot, slot, send2.at[d], recv2.at[d], sibling)
        copy.start()
        sends.append(copy)
    for d in range(chips):
        source = ((chip - d + chips) % chips) * 2 + (1 - core)
        remote(w_ref, out_ref.at[source], send2.at[d], recv2.at[d], sibling).wait_recv()

    @pl.when(mine)
    def _():
        for d in range(1, planes):
            source = (tp + d) % planes
            remote(o_ref, col_ref.at[source], sendz, recvz.at[source], (me, source)).wait_recv()

    @pl.when(jnp.logical_not(mine))
    def _():
        hop.wait_send()

    wait_line()
    for copy in sends:
        copy.wait_send()
    own.wait()
    kept.wait()


def gather_rows(weight, out_weight, tokens, rows):
    count, planes = lax.axis_size("stream"), lax.axis_size("tp")
    chips = count // 2
    dma = pltpu.SemaphoreType.DMA
    anywhere = pl.BlockSpec(memory_space=pl.ANY)
    return pl.pallas_call(
        functools.partial(gather_kernel, chips, planes, rows),
        out_shape=(
            jax.ShapeDtypeStruct((count,) + weight.shape, weight.dtype),
            jax.ShapeDtypeStruct((planes,) + out_weight.shape, out_weight.dtype),
            jax.ShapeDtypeStruct((rows, planes * tokens.shape[1]), tokens.dtype),
        ),
        in_specs=[anywhere] * 3,
        out_specs=(anywhere,) * 3,
        scratch_shapes=[dma((chips,))] * 4 + [dma] + [dma((planes,))] * 3 + [dma((3,))],
        compiler_params=pltpu.CompilerParams(collective_id=0, has_side_effects=True),
        cost_estimate=pl.CostEstimate(flops=0, bytes_accessed=200_000_000, transcendentals=0),
        name="gather_rows",
    )(weight, out_weight, tokens)


def spread_kernel(
    count, planes, col_ref, h_ref, out_ref, heads_ref, sendx, recvx, sends, recvs, sendh, recvh, local
):
    me = lax.axis_index("stream")
    tp = lax.axis_index("tp")
    chips, per = count // 2, count // planes
    chip, core = me // 2, me % 2
    sibling = (chip * 2 + (1 - core), tp)
    peers = [(((chip + d) % chips) * 2 + core, tp) for d in range(1, chips)]
    column = [(me, (tp + d) % planes) for d in range(1, planes)]
    greet(peers + [sibling] + column)
    owner, place = me // per, me % per
    start_line, wait_line = line_copies(planes, h_ref, heads_ref, sendh, recvh, local.at[1])
    start_line()
    mine = owner == tp

    @pl.when(mine)
    def _():
        for d in range(1, chips):
            remote(col_ref, out_ref.at[place], sendx.at[d], recvx.at[place // 2], peers[d - 1]).start()
        own = pltpu.make_async_copy(col_ref, out_ref.at[place], local.at[0])
        own.start()
        own.wait()

    for i in range(per // 2):
        slot = out_ref.at[2 * i + core]
        source = tp * per + 2 * i + core

        @pl.when(source != me)
        def _():
            remote(slot, slot, sendx.at[0], recvx.at[i], sibling).wait_recv()

        remote(slot, slot, sends.at[i], recvs.at[i], sibling).start()
    for i in range(per // 2):
        other = out_ref.at[2 * i + (1 - core)]
        remote(other, other, sends.at[i], recvs.at[i], sibling).wait_recv()
    for i in range(per // 2):
        slot = out_ref.at[2 * i + core]
        remote(slot, slot, sends.at[i], recvs.at[i], sibling).wait_send()

    @pl.when(mine)
    def _():
        for d in range(1, chips):
            remote(col_ref, out_ref.at[place], sendx.at[d], recvx.at[place // 2], peers[d - 1]).wait_send()

    wait_line()


def spread_columns(columns, hidden):
    count, planes = lax.axis_size("stream"), lax.axis_size("tp")
    chips, per = count // 2, count // planes
    dma = pltpu.SemaphoreType.DMA
    return pl.pallas_call(
        functools.partial(spread_kernel, count, planes),
        out_shape=(
            jax.ShapeDtypeStruct((per,) + columns.shape, columns.dtype),
            jax.ShapeDtypeStruct((hidden.shape[0], planes * hidden.shape[1]), hidden.dtype),
        ),
        in_specs=[pl.BlockSpec(memory_space=pl.ANY)] * 2,
        out_specs=(pl.BlockSpec(memory_space=pl.ANY),) * 2,
        scratch_shapes=[dma((chips,))] + [dma((per // 2,))] * 3 + [dma((planes,))] * 2 + [dma((2,))],
        compiler_params=pltpu.CompilerParams(collective_id=1, has_side_effects=True),
        cost_estimate=pl.CostEstimate(flops=0, bytes_accessed=200_000_000, transcendentals=0),
        name="spread_columns",
    )(columns, hidden)


def halves(x):
    high = x.astype(jnp.bfloat16)
    return high, (x - high.astype(jnp.float32)).astype(jnp.bfloat16)


def product(a, b, left, right):
    return lax.dot_general(a, b, (((left,), (right,)), ((), ())), preferred_element_type=jnp.float32)


def attend_kernel(first, heads, valid_ref, proj_ref, decay_ref, moved_ref, *refs):
    hidden_ref, updated_ref = refs[-2:]
    length, width = WINDOW_LENGTH, heads * HD
    count = valid_ref[first + pl.program_id(0)]
    column = lax.broadcasted_iota(jnp.int32, (length, 1), 0)
    live = (column < count).astype(jnp.float32)
    rows = lax.broadcasted_iota(jnp.int32, (length, length), 0)
    cols = lax.broadcasted_iota(jnp.int32, (length, length), 1)
    live_row = lax.broadcasted_iota(jnp.int32, (heads, length), 1) < count
    decay = jnp.where(live_row, decay_ref[...], 0.0)
    ones = (rows <= cols).astype(jnp.float32)
    across = lax.dot_general(
        decay,
        ones,
        (((1,), (0,)), ((), ())),
        precision=lax.Precision.HIGHEST,
        preferred_element_type=jnp.float32,
    )
    down = across.T
    causal = rows >= cols
    for pair in range(heads // 2):
        block = slice(pair * 2 * HD, (pair + 1) * 2 * HD)

        def active(part):
            x = proj_ref[:, part * width + block.start : part * width + block.stop]
            return x * jax.nn.sigmoid(x)

        queries = active(0).astype(jnp.bfloat16)
        keys = (active(1) * live).astype(jnp.bfloat16)
        values = (active(2) * live).astype(jnp.bfloat16)
        gates = jax.nn.sigmoid(proj_ref[:, 3 * width + block.start : 3 * width + block.stop]) * live
        outs = []
        for side in range(2):
            h = 2 * pair + side
            lanes = slice(side * HD, (side + 1) * HD)
            q, k, v = queries[:, lanes], keys[:, lanes], values[:, lanes]
            along, above = down[:, h : h + 1], across[h : h + 1, :]
            last = across[h : h + 1, length - 1 :]
            weights = jnp.where(causal, jnp.exp(jnp.minimum(along - above, 0.0)), 0.0)
            probs = (product(q, k, 1, 1) * weights).astype(jnp.bfloat16)
            old = moved_ref[0, h]
            high, low = halves(old)
            carried = product(q, high, 1, 0) + product(q, low, 1, 0)
            attended = product(probs, v, 1, 0) + carried * jnp.exp(along)
            high, low = halves(k.astype(jnp.float32) * jnp.exp(last - along))
            updated_ref[0, h] = jnp.exp(last) * old + (product(high, v, 0, 0) + product(low, v, 0, 0))
            mean_square = jnp.mean(attended * attended, axis=1, keepdims=True)
            outs.append(attended * lax.rsqrt(mean_square + 1e-05))
        hidden_ref[:, block] = (jnp.concatenate(outs, axis=1) * gates).astype(jnp.bfloat16)


def attend(projected, valid, log_decay, moved, first, part, earlier):
    streams, heads = moved.shape[:2]
    length, width = WINDOW_LENGTH, heads * HD
    in_specs = [
        pl.BlockSpec((length, 4 * width), lambda i, v: (i, 0)),
        pl.BlockSpec((heads, length), lambda i, v: (0, first + i)),
        pl.BlockSpec((1, heads, HD, HD), lambda i, v: (first + i, 0, 0, 0)),
    ]
    operands = [projected, log_decay, moved]
    aliases = {}
    if earlier is not None:
        in_specs.append(pl.BlockSpec(memory_space=pl.ANY))
        operands.append(earlier)
        aliases = {4: 1}
    return pl.pallas_call(
        functools.partial(attend_kernel, first, heads),
        out_shape=(
            jax.ShapeDtypeStruct((part * length, width), jnp.bfloat16),
            jax.ShapeDtypeStruct(moved.shape, jnp.float32),
        ),
        grid_spec=pltpu.PrefetchScalarGridSpec(
            num_scalar_prefetch=1,
            grid=(part,),
            in_specs=in_specs,
            out_specs=(
                pl.BlockSpec((length, width), lambda i, v: (i, 0)),
                pl.BlockSpec((1, heads, HD, HD), lambda i, v: (first + i, 0, 0, 0)),
            ),
        ),
        input_output_aliases=aliases,
        cost_estimate=pl.CostEstimate(flops=0, bytes_accessed=40_000_000, transcendentals=0),
        name="attend",
    )(valid, *operands)


def body(tokens, qkv_weight, gate_weight, out_weight, log_decay, states, dest_slot, valid):
    streams, heads = states.shape[:2]
    width = heads * HD
    lead, tail = streams // 4, 5 * streams // 12
    middle = (streams - lead - tail) // 2
    parts = [lead, middle, streams - lead - tail - middle, tail]
    firsts = [sum(parts[:c]) for c in range(len(parts))]
    features = [None]
    for first, part in zip(firsts[1:], parts[1:]):
        piece = tokens[first * WINDOW_LENGTH : (first + part) * WINDOW_LENGTH]
        features.append(lax.all_gather(piece, "tp", axis=1, tiled=True))
    local = jnp.concatenate([qkv_weight.reshape(-1, 3 * width), gate_weight], axis=1)
    moved = move_states(states, dest_slot)
    weights, columns, features[0] = gather_rows(local, out_weight, tokens, lead * WINDOW_LENGTH)
    weights = weights.reshape(-1, 4 * width)
    gathered, updated = [], None
    for c, part in enumerate(parts):
        projected = jnp.dot(features[c], weights, preferred_element_type=jnp.float32)
        hidden, updated = attend(projected, valid, log_decay, moved, firsts[c], part, updated)
        if c + 1 < len(parts):
            gathered.append(lax.all_gather(hidden, "tp", axis=1, tiled=True))
    spread, heads_last = spread_columns(columns, hidden)
    gathered.append(heads_last)
    per = spread.shape[0]
    full_rows = spread.reshape(per, -1, out_weight.shape[1]).transpose(1, 0, 2)
    full_rows = full_rows.reshape(full_rows.shape[0], -1)
    mixed = [
        jnp.dot(part_heads, full_rows, preferred_element_type=jnp.float32).astype(jnp.bfloat16)
        for part_heads in gathered
    ]
    return (jnp.concatenate(mixed, axis=0), updated)


def solution(mesh):
    return jax.shard_map(
        body,
        mesh=mesh,
        in_specs=(
            P("stream", "tp"),
            P("stream", None, "tp"),
            P("stream", "tp"),
            P("tp", "stream"),
            P("tp", "stream"),
            P("stream", "tp", None, None),
            P("stream"),
            P("stream"),
        ),
        out_specs=(P("stream", "tp"), P("stream", "tp", None, None)),
        check_vma=False,
    )
```
